256 devices in a mesh: expert: 64 (over z, x, core), dp: 4 (over y).
Axes of the slice: x: 4, y: 4, z: 8, core: 2. Of those that a mesh axis runs over, the one named last changes fastest.
Arguments:
- tokens: bfloat16 [32768, 2048], P(('expert', 'dp')), may hold values from -6 to 6
- expert_ids: int32 [32768, 2], P(('expert', 'dp')), may hold values from 0 to 63, all different within a row; in each aligned block of 128 rows (0 to 127, 128 to 255, ...) at most 6 rows name the same one
- gate_scores: float32 [32768, 2], P(('expert', 'dp')), may hold values from 0.2 to 1
- gate_proj: bfloat16 [64, 768, 2048], P('expert', 'dp'), may hold values from -0.125 to 0.125
- up_proj: bfloat16 [64, 768, 2048], P('expert', 'dp'), may hold values from -0.125 to 0.125
- down_proj: bfloat16 [64, 768, 2048], P('expert', 'dp'), may hold values from -0.21875 to 0.21875
- out_grad: bfloat16 [32768, 2048], P(('expert', 'dp')), may hold values from -0.59765625 to 0.59765625
Outputs:
- output: bfloat16 [32768, 2048], P(('expert', 'dp'))
- d_tokens: bfloat16 [32768, 2048], P(('expert', 'dp'))
- d_scores: float32 [32768, 2], P(('expert', 'dp'))
- d_gate_proj: bfloat16 [64, 768, 2048], P('expert', 'dp')
- d_up_proj: bfloat16 [64, 768, 2048], P('expert', 'dp')
- d_down_proj: bfloat16 [64, 768, 2048], P('expert', 'dp')
The draws below stay inside these ranges and needn't reach their ends.
Inputs may be any that keep to these rules, and one draw needn't show every extreme that they name: `expert_ids`: each token names 2 different experts. Among the routes of one device's 128 tokens no expert is named more than 6 times, and in some devices' blocks some expert is named exactly 6 times.
All inputs are finite; a program needn't handle non-finite values.
Results may differ from the reference program's by a relative error of at most 0.014.
Values may be sent and summed in bfloat16 or wider, within the bound.
A program may use at most 128 MiB of HBM per device.

```python
import math
import jax
import jax.numpy as jnp
import numpy as np
from jax import lax

D = 2048
FF = 768
TOP = 2
TOK_DEV = 128
EXPERTS = 64
CAP = 6
TOKENS = 32768
N_EXPERT = 64
N_DP = 4


def shard_levels(own_key, dims, shards, low, high):
    gain = 1.0
    for dim, parts in shards:
        heights = jax.random.uniform(jax.random.fold_in(jax.random.fold_in(own_key, 6), dim), (parts,), jnp.float32, low / len(shards), high / len(shards))
        gain = gain * jnp.repeat(jnp.exp(heights), dims[dim] // parts).reshape((-1,) + (1,) * (len(dims) - 1 - dim))
    return gain


def assign_block(stream_key, own, number, rows, number_of, top, limit, skew):
    order = jax.random.permutation(stream_key, number_of)
    packed, usual = shares(number_of, rows * top, limit, skew, True), shares(number_of, rows * top, limit, skew, False)
    places = jnp.arange(number_of)

    def named(lengths, turn):
        used = int((lengths > 0).sum())
        fixed = max(1, used // 4)
        moved = fixed + (places - fixed + turn * (used - fixed)) % max(1, number_of - fixed)
        return jnp.zeros((number_of,), jnp.int32).at[order[jnp.where(places < fixed, places, moved)]].set(jnp.asarray(lengths, jnp.int32))

    lengths = jnp.where(number % 4 == 0, named(packed, number // 4), named(usual, number - number // 4 - 1))
    mixed = jax.random.permutation(jax.random.fold_in(own, 3), number_of)
    source_of, sink = mixed[0:number_of // 2 * 2:2], mixed[1:number_of // 2 * 2:2]
    room = jnp.minimum(lengths[source_of] - 1, limit - lengths[sink]) // 2
    room = jnp.where((source_of == order[0]) | (sink == order[0]) | (lengths[sink] == 0), 0, jnp.maximum(room, 0))
    moved = jax.random.randint(jax.random.fold_in(own, 4), (number_of // 2,), 0, 1 << 20) % (room + 1)
    lengths = lengths.at[source_of].add(-moved).at[sink].add(moved)
    members = jnp.searchsorted(jnp.cumsum(lengths), jnp.arange(rows * top), side="right").astype(jnp.int32)
    listing = members.reshape(top, rows).T
    listing = listing[jax.random.permutation(jax.random.fold_in(own, 1), rows)]
    turn = jax.random.randint(jax.random.fold_in(own, 2), (rows, 1), 0, top)
    return jnp.take_along_axis(listing, (jnp.arange(top)[None, :] + turn) % top, axis=1)


def shares(count, total, limit, skew, full):
    weights = [(1 << 20) // math.isqrt(grade ** skew) + 1 for grade in range(1, count + 1)]
    largest = limit if full else min(limit, max(-(-total // count), total * weights[0] // sum(weights)))
    least = 1 if total - largest >= count - 1 else 0
    holding, rest = [largest] + [least] * (count - 1), total - largest - least * (count - 1)
    while rest > 0:
        candidates = [i for i in range(1, count) if holding[i] < largest] or [i for i in range(1, count) if holding[i] < limit]
        mass, budget = sum([weights[i] for i in candidates]), rest
        for i in candidates:
            more = min(limit - holding[i], max(1, budget * weights[i] // mass), rest)
            holding[i] = holding[i] + more
            rest = rest - more
    return np.array(holding)


def noise(key, shape, spread, most, split=(), held_as=jnp.bfloat16):
    result = spread * jax.random.normal(key, shape, jnp.float32)
    if split:
        result = result * shard_levels(key, shape, split, -0.22, 0.18)
    return jnp.clip(result, -most, most).astype(held_as)


def setup_inputs(seed: int = 0) -> dict:
    key_list = jax.random.split(jax.random.key(seed), 8)
    tokens = noise(key_list[0], (TOKENS, D), 1.0, 6.0, ((0, 256),))
    expert_ids_keys = jax.random.split(jax.random.fold_in(key_list[1], 1), TOKENS // TOK_DEV)
    expert_ids_turns = jax.random.permutation(jax.random.fold_in(key_list[1], 3), TOKENS // TOK_DEV)
    expert_ids = jax.vmap(lambda own, number: assign_block(jax.random.fold_in(key_list[1], 2), own, number, TOK_DEV, EXPERTS, TOP, CAP, 2))(expert_ids_keys, expert_ids_turns).reshape((TOKENS, TOP))
    gate_scores = jnp.clip(0.2 + 0.8 * jax.random.uniform(key_list[2], (TOKENS, TOP), jnp.float32) ** shard_levels(key_list[2], (TOKENS, TOP), ((0, 256),), -0.2, 0.2), 0.2, 1.0)
    gate_proj = noise(key_list[3], (EXPERTS, FF, D), D ** -0.5, 0.125, ((0, 64), (1, 4)))
    up_proj = noise(key_list[4], (EXPERTS, FF, D), D ** -0.5, 0.125, ((0, 64), (1, 4)))
    down_proj = noise(key_list[5], (EXPERTS, FF, D), FF ** -0.5, 0.21875, ((0, 64), (1, 4)))
    out_grad = noise(key_list[6], (TOKENS, D), 0.1, 0.59765625, ((0, 256),))
    return {"tokens": tokens, "expert_ids": expert_ids, "gate_scores": gate_scores, "gate_proj": gate_proj, "up_proj": up_proj, "down_proj": down_proj, "out_grad": out_grad}


def silu_parts(preact):
    logistic = jax.nn.sigmoid(preact)
    return preact * logistic, logistic * (1.0 + preact * (1.0 - logistic))


def regroup(values):
    shaped = values.reshape(N_EXPERT, N_DP, CAP, values.shape[-1])
    return jnp.transpose(shaped, (1, 0, 2, 3)).reshape(N_DP, N_EXPERT * CAP, values.shape[-1])


def per_group(left_rows, right_rows):
    left_rows = regroup(left_rows).astype(jnp.float32)
    right_rows = regroup(right_rows).astype(jnp.float32)
    partial_value = jnp.einsum("gsf,gsd->gfd", left_rows, right_rows)
    rounded = lax.optimization_barrier(partial_value.astype(jnp.bfloat16))
    return jnp.sum(rounded.astype(jnp.float32), axis=0).astype(jnp.bfloat16)


def reference(tokens, expert_ids, gate_scores, gate_proj, up_proj, down_proj, out_grad):
    devices = N_EXPERT * N_DP
    pair_total = TOKENS * TOP
    block_ids = expert_ids.reshape(devices, TOK_DEV * TOP)
    onehot = (block_ids[:, :, None] == jnp.arange(EXPERTS, dtype=jnp.int32)[None, None, :]).astype(jnp.int32)
    position = jnp.sum(jnp.cumsum(onehot, axis=1) * onehot, axis=2) - 1
    source = jnp.arange(devices, dtype=jnp.int32)[:, None]
    target = ((block_ids * devices + source) * CAP + position).reshape(-1).astype(jnp.int32)
    slot_table = jnp.full((EXPERTS * devices * CAP,), pair_total, dtype=jnp.int32)
    slot_table = slot_table.at[target].set(jnp.arange(pair_total, dtype=jnp.int32))
    padded_tokens = jnp.concatenate([tokens, jnp.zeros((1, D), tokens.dtype)], axis=0)
    padded_grad = jnp.concatenate([out_grad, jnp.zeros((1, D), out_grad.dtype)], axis=0)
    padded_scores = jnp.concatenate([gate_scores.reshape(-1), jnp.zeros((1,), jnp.float32)])

    def one_expert(operands):
        slot_ids, gate_w, up_w, down_w = operands
        token_ids = slot_ids // TOP
        gathered = padded_tokens[token_ids]
        gate_pre = jnp.dot(gathered, gate_w.T, preferred_element_type=jnp.float32)
        up_pre = jnp.dot(gathered, up_w.T, preferred_element_type=jnp.float32)
        activated, silu_slope = silu_parts(gate_pre)
        hidden = (activated * up_pre).astype(jnp.bfloat16)
        expert_out = jnp.dot(hidden, down_w, preferred_element_type=jnp.float32).astype(jnp.bfloat16)
        out_cot = (padded_scores[slot_ids][:, None] * padded_grad[token_ids].astype(jnp.float32)).astype(jnp.bfloat16)
        hidden_grad = jnp.dot(out_cot, down_w.T, preferred_element_type=jnp.float32)
        gate_grad = (hidden_grad * up_pre * silu_slope).astype(jnp.bfloat16)
        up_grad = (hidden_grad * activated).astype(jnp.bfloat16)
        input_grad = (jnp.dot(gate_grad, gate_w, preferred_element_type=jnp.float32)
                      + jnp.dot(up_grad, up_w, preferred_element_type=jnp.float32)).astype(jnp.bfloat16)
        return (expert_out, input_grad, per_group(gate_grad, gathered),
                per_group(up_grad, gathered), per_group(hidden, out_cot))

    expert_out, input_grad, d_gate_proj, d_up_proj, d_down_proj = lax.map(
        one_expert, (slot_table.reshape(EXPERTS, devices * CAP), gate_proj, up_proj, down_proj))
    flat_slots = slot_table.reshape(-1)
    pair_out = jnp.zeros((pair_total + 1, D), jnp.bfloat16).at[flat_slots].set(expert_out.reshape(-1, D))[:pair_total]
    pair_input = jnp.zeros((pair_total + 1, D), jnp.bfloat16).at[flat_slots].set(input_grad.reshape(-1, D))[:pair_total]
    pair_out = pair_out.reshape(TOKENS, TOP, D).astype(jnp.float32)
    output = jnp.sum(gate_scores[:, :, None] * pair_out, axis=1).astype(jnp.bfloat16)
    d_scores = jnp.sum(out_grad.astype(jnp.float32)[:, None, :] * pair_out, axis=2)
    d_tokens = jnp.sum(pair_input.reshape(TOKENS, TOP, D).astype(jnp.float32), axis=1).astype(jnp.bfloat16)
    return output, d_tokens, d_scores, d_gate_proj, d_up_proj, d_down_proj
```

```python
import functools

import jax
import jax.numpy as jnp
import numpy as np
from jax import lax
from jax.experimental import pallas as pl
from jax.experimental.pallas import tpu as pltpu
from jax.sharding import PartitionSpec as P

MESH = pl.DeviceIdType.MESH
D, FF, TOK, CAP, NEXP, NDP = 2048, 768, 128, 6, 64, 4
SH = FF // NDP
HALF = SH // 2
SLOTS = NEXP * CAP
LANES = 512
PIECES = D // LANES
PEER = 2 * PIECES * CAP
GRP = 8
GROWS = GRP * PEER
GSLOTS = GRP * CAP
BF, F32, I32 = jnp.bfloat16, jnp.float32, jnp.int32
FCHUNK = 256

_r = np.arange(GROWS)
_peer, _kind, _piece, _slot = _r // PEER, _r % PEER // (PIECES * CAP), _r % (PIECES * CAP) // CAP, _r % CAP
BASE = (_peer * CAP + _slot).astype(np.int32)[:, None]
ISCOT = (_kind == 1).astype(np.float32)[:, None]
BLOCKMASK = np.repeat(
    (_kind * PIECES + _piece)[:, None] == np.arange(2 * PIECES)[None, :], TOK, axis=1
).astype(np.float32)
_dest = (_kind * PIECES + _piece) * GSLOTS + _peer * CAP + _slot
PERM = np.zeros((GROWS, GROWS), np.float32)
PERM[_dest, _r] = 1.0


def dot(a, b, ca=1, cb=0):
    return lax.dot_general(a, b, (((ca,), (cb,)), ((), ())), preferred_element_type=F32)


def place():
    me, y = lax.axis_index("expert"), lax.axis_index("dp")
    return me, y, me // 8, (me // 2) % 4, me % 2


def barrier(sems):
    me, y, z, x, c = place()
    at = lambda z, x, c: z * 8 + x * 2 + c
    zs = [at((z + 1) % 8, x, c), at((z + 7) % 8, x, c)]
    xs = [at(z, (x + 1) % 4, c), at(z, (x + 3) % 4, c)]
    cs = [at(z, x, 1 - c)]
    bar = pltpu.get_barrier_semaphore()

    def tell(sem, devices):
        for d in devices:
            pl.semaphore_signal(sem, inc=1, device_id=d, device_id_type=MESH)

    tell(bar, [(d, y) for d in zs + xs + cs] + [(me, (y + 1) % 4), (me, (y + 3) % 4)])
    pl.semaphore_wait(bar, 7)
    for i, group in enumerate((zs, zs, zs, xs, xs, cs)):
        tell(sems.at[i], [(d, y) for d in group])
        pl.semaphore_wait(sems.at[i], len(group))


def remote(src, dst, send, recv, device):
    return pltpu.make_async_remote_copy(src, dst, send, recv, device_id=device, device_id_type=MESH)


def start_exchange(src, dst, send, recv, local):
    me, y, z, x, c = place()
    own = pltpu.make_async_copy(src.at[me], dst.at[me], local)
    own.start()

    def one(k, carry):
        peer = ((z + k // 8) % 8) * 8 + ((x + (k // 2) % 4) % 4) * 2 + (c + k % 2) % 2
        remote(src.at[peer], dst.at[me], send, recv, (peer, y)).start()
        return carry

    lax.fori_loop(1, NEXP, one, 0)
    return own


def finish_exchange(src, dst, send, recv, own):
    n = NEXP - 1
    pltpu.make_async_copy(dst.at[pl.ds(0, n)], dst.at[pl.ds(0, n)], recv).wait()
    pltpu.make_async_copy(src.at[pl.ds(0, n)], src.at[pl.ds(0, n)], send).wait()
    own.wait()


def targets_row(ids, ids_t):
    before = lax.broadcasted_iota(I32, (TOK, TOK), 0) < lax.broadcasted_iota(I32, (TOK, TOK), 1)
    out = []
    for k in range(2):
        mine = ids_t[k : k + 1, :]
        same = (ids[:, 0:1] == mine).astype(F32) + (ids[:, 1:2] == mine).astype(F32)
        pos = jnp.sum(jnp.where(before, same, 0.0), axis=0, keepdims=True)
        out.append(mine * CAP + pos.astype(I32))
    return out


def targets_col(ids, ids_t):
    before = lax.broadcasted_iota(I32, (TOK, TOK), 1) < lax.broadcasted_iota(I32, (TOK, TOK), 0)
    out = []
    for k in range(2):
        mine = ids[:, k : k + 1]
        same = (ids_t[0:1, :] == mine).astype(F32) + (ids_t[1:2, :] == mine).astype(F32)
        pos = jnp.sum(jnp.where(before, same, 0.0), axis=1, keepdims=True)
        out.append(mine * CAP + pos.astype(I32))
    return out


def pack_kernel(tok, grad, ids, ids_t, sc_t, base, iscot, mask, out, table):
    for piece in range(PIECES):
        lanes = slice(piece * LANES, (piece + 1) * LANES)
        table[piece * TOK : (piece + 1) * TOK, :] = tok[:, lanes]
        table[(PIECES + piece) * TOK : (PIECES + piece + 1) * TOK, :] = grad[:, lanes]
    t0, t1 = targets_row(ids[...], ids_t[...])
    s0, s1 = sc_t[0:1, :], sc_t[1:2, :]

    def one(g, carry):
        slot = base[...] + g * GSLOTS
        h0, h1 = t0 == slot, t1 == slot
        score = jnp.sum(jnp.where(h0, s0, 0.0) + jnp.where(h1, s1, 0.0), axis=1, keepdims=True)
        scale = jnp.where(iscot[...] > 0.0, score, 1.0)
        hit = (h0.astype(F32) + h1.astype(F32)).astype(BF)
        pick = jnp.concatenate([hit] * (2 * PIECES), axis=1) * mask[...]
        rows = dot(pick, table[...]) * scale
        out[pl.ds(pl.multiple_of(g * GROWS, GROWS), GROWS), :] = rows.astype(BF)
        return carry

    lax.fori_loop(0, NEXP // GRP, one, 0)


def dispatch_kernel(x, wg, wu, wd, out, fg, fu, fd, bsem, xs, xr, loc, ws, wr):
    me, y, *_ = place()
    up, dn = (y + 1) % 4, (y + 3) % 4
    shards, fulls = (wg, wu, wd), (fg, fu, fd)
    at = lambda ref, who, off, n: ref.at[pl.ds(pl.multiple_of(who * SH + off, 32), n)]
    mine = [pltpu.make_async_copy(s, at(f, y, 0, SH), loc.at[1 + m]) for m, (s, f) in enumerate(zip(shards, fulls))]
    for q in mine:
        q.start()
    barrier(bsem)
    first, relay = [], []
    for m, (s, f) in enumerate(zip(shards, fulls)):
        for way, to in enumerate((up, dn)):
            q = remote(s, at(f, y, 0, SH), ws.at[way, m], wr.at[way, m], (me, to))
            q.start()
            first.append((m, way, q))
    own = start_exchange(x, out, xs, xr, loc.at[0])
    for m, way, q in first:
        q.wait_recv()
        part = at(fulls[m], dn if way == 0 else up, way * HALF, HALF)
        r = remote(part, part, ws.at[2 + way, m], wr.at[2 + way, m], (me, up if way == 0 else dn))
        r.start()
        relay.append(r)
    for q in relay:
        q.wait()
    for _, _, q in first:
        q.wait_send()
    for q in mine:
        q.wait()
    finish_exchange(x, out, xs, xr, own)


def unpack_rows(perm, rows, first, second):
    def one(g, carry):
        z = dot(perm[...], rows[pl.ds(pl.multiple_of(g * GROWS, GROWS), GROWS), :]).astype(BF)
        at = pl.ds(pl.multiple_of(g * GSLOTS, GSLOTS), GSLOTS)
        for kind, ref in enumerate((first, second)):
            for piece in range(PIECES):
                o = (kind * PIECES + piece) * GSLOTS
                ref[at, piece * LANES : (piece + 1) * LANES] = z[o : o + GSLOTS]
        return carry

    lax.fori_loop(0, NEXP // GRP, one, 0)


def pack_rows(perm, out, first, second):
    def one(g, carry):
        at = pl.ds(pl.multiple_of(g * GSLOTS, GSLOTS), GSLOTS)
        z = [
            ref[at, piece * LANES : (piece + 1) * LANES].astype(BF)
            for ref in (first, second)
            for piece in range(PIECES)
        ]
        packed = dot(perm[...], jnp.concatenate(z, axis=0), 0, 0)
        out[pl.ds(pl.multiple_of(g * GROWS, GROWS), GROWS), :] = packed.astype(BF)
        return carry

    lax.fori_loop(0, NEXP // GRP, one, 0)


def expert_kernel(rows, perm, wg, wu, wd, out, dg, du, dd, xt, xc, acc_o, acc_i):
    step = pl.program_id(0)

    @pl.when(step == 0)
    def _():
        unpack_rows(perm, rows, xt, xc)

    gate = dot(xt[...], wg[...], 1, 1)
    up = dot(xt[...], wu[...], 1, 1)
    hg = dot(xc[...], wd[...], 1, 1)
    s = jax.nn.sigmoid(gate)
    act = gate * s
    hidden = (act * up).astype(BF)
    ggrad = (hg * up * (s * (1.0 + gate * (1.0 - s)))).astype(BF)
    ugrad = (hg * act).astype(BF)
    dg[...] = dot(ggrad, xt[...], 0, 0).astype(BF)
    du[...] = dot(ugrad, xt[...], 0, 0).astype(BF)
    dd[...] = dot(hidden, xc[...], 0, 0).astype(BF)
    o = dot(hidden, wd[...])
    i = dot(ggrad, wg[...]) + dot(ugrad, wu[...])

    @pl.when(step == 0)
    def _():
        acc_o[...] = o
        acc_i[...] = i

    @pl.when(step > 0)
    def _():
        acc_o[...] += o
        acc_i[...] += i

    @pl.when(step == FF // FCHUNK - 1)
    def _():
        pack_rows(perm, out, acc_o, acc_i)


def return_kernel(
    x, pg, pu, pd, out, og, ou, od, bsem, xs, xr, loc, rel, add, summed, frm, own_w, rs_s, rs_r
):
    me, y, *_ = place()
    up, dn, far = (y + 1) % 4, (y + 3) % 4, (y + 2) % 4
    parts = (pg, pu, pd)
    at = lambda ref, who, off, n: ref.at[pl.ds(pl.multiple_of(who * SH + off, 32), n)]
    loads = []
    for m, p in enumerate(parts):
        qs = [
            pltpu.make_async_copy(at(p, up, 0, HALF), add.at[0, m], loc.at[1 + m]),
            pltpu.make_async_copy(at(p, dn, HALF, HALF), add.at[1, m], loc.at[4 + m]),
            pltpu.make_async_copy(at(p, y, 0, SH), own_w.at[m], loc.at[7 + m]),
        ]
        for q in qs:
            q.start()
        loads.append(qs)
    barrier(bsem)
    tos = (up, dn)
    relays, directs, sums = [], [], []
    for m, p in enumerate(parts):
        for way in range(2):
            q = remote(at(p, far, way * HALF, HALF), rel.at[way, m], rs_s.at[way, m], rs_r.at[way, m], (me, tos[way]))
            q.start()
            relays.append((m, way, q))
    for m, p in enumerate(parts):
        for way in range(2):
            off = (1 - way) * HALF
            q = remote(
                at(p, tos[way], off, HALF),
                frm.at[way, m, pl.ds(off, HALF)],
                rs_s.at[2 + way, m],
                rs_r.at[2 + way, m],
                (me, tos[way]),
            )
            q.start()
            directs.append(q)
    own = start_exchange(x, out, xs, xr, loc.at[0])
    for m, way, q in relays:
        q.wait_recv()
        loads[m][way].wait()

        def add_rows(r, carry):
            rows = pl.ds(pl.multiple_of(r * 32, 32), 32)
            total = rel[way, m, rows, :].astype(F32) + add[way, m, rows, :].astype(F32)
            summed[way, m, rows, :] = total.astype(BF)
            return carry

        lax.fori_loop(0, HALF // 32, add_rows, 0)
        off = way * HALF
        s = remote(
            summed.at[way, m], frm.at[way, m, pl.ds(off, HALF)], rs_s.at[4 + way, m], rs_r.at[4 + way, m], (me, tos[way])
        )
        s.start()
        sums.append(s)
    for q in directs:
        q.wait()
    for q in sums:
        q.wait()
    for m, (_, ref) in enumerate(zip(parts, (og, ou, od))):
        loads[m][2].wait()

        def final(r, carry):
            rows = pl.ds(pl.multiple_of(r * 32, 32), 32)
            total = own_w[m, rows, :].astype(F32) + frm[0, m, rows, :].astype(F32)
            ref[rows, :] = (total + frm[1, m, rows, :].astype(F32)).astype(BF)
            return carry

        lax.fori_loop(0, SH // 32, final, 0)
    for _, _, q in relays:
        q.wait_send()
    finish_exchange(x, out, xs, xr, own)


def combine_kernel(rows, perm, grad, ids, ids_t, sc, out, dtok, dsc, xo, xi):
    unpack_rows(perm, rows, xo, xi)
    t0, t1 = targets_col(ids[...], ids_t[...])
    slot = lax.broadcasted_iota(I32, (TOK, SLOTS), 1)
    g0 = (t0 == slot).astype(F32).astype(BF)
    g1 = (t1 == slot).astype(F32).astype(BF)
    both = g0 + g1
    s0, s1 = sc[:, 0:1], sc[:, 1:2]
    d0 = jnp.zeros((TOK, 1), F32)
    d1 = jnp.zeros((TOK, 1), F32)
    for piece in range(PIECES):
        lanes = slice(piece * LANES, (piece + 1) * LANES)
        p0 = dot(g0, xo[:, lanes])
        p1 = dot(g1, xo[:, lanes])
        og = grad[:, lanes].astype(F32)
        out[:, lanes] = (s0 * p0 + s1 * p1).astype(BF)
        d0 += jnp.sum(og * p0, axis=1, keepdims=True)
        d1 += jnp.sum(og * p1, axis=1, keepdims=True)
        dtok[:, lanes] = dot(both, xi[:, lanes]).astype(BF)
    dsc[...] = jnp.concatenate([d0, d1], axis=1)


def shards(tokens, expert_ids, gate_scores, gate_proj, up_proj, down_proj, out_grad):
    sd = jax.ShapeDtypeStruct
    vm = pl.BlockSpec(memory_space=pltpu.VMEM)
    anyw = pl.BlockSpec(memory_space=pl.ANY)
    dma, reg = pltpu.SemaphoreType.DMA, pltpu.SemaphoreType.REGULAR
    ids_t, sc_t = expert_ids.T, gate_scores.T
    perm = jnp.asarray(PERM, BF)
    big = NEXP * PEER
    packed = pl.pallas_call(
        pack_kernel,
        name="pack",
        out_shape=sd((big, LANES), BF),
        in_specs=[vm] * 8,
        out_specs=vm,
        scratch_shapes=[pltpu.VMEM((2 * PIECES * TOK, LANES), BF)],
        compiler_params=pltpu.CompilerParams(vmem_limit_bytes=48 << 20),
    )(tokens, out_grad, expert_ids, ids_t, sc_t, jnp.asarray(BASE), jnp.asarray(ISCOT), jnp.asarray(BLOCKMASK, BF))
    wg, wu, wd = gate_proj[0], up_proj[0], down_proj[0]
    received, fg, fu, fd = pl.pallas_call(
        dispatch_kernel,
        name="dispatch",
        out_shape=(sd((NEXP, PEER, LANES), BF),) + (sd((FF, D), BF),) * 3,
        in_specs=[anyw] * 4,
        out_specs=(anyw,) * 4,
        scratch_shapes=[reg((6,)), dma, dma, dma((4,)), dma((4, 3)), dma((4, 3))],
        compiler_params=pltpu.CompilerParams(collective_id=1, has_side_effects=True, vmem_limit_bytes=16 << 20),
    )(packed.reshape(NEXP, PEER, LANES), wg, wu, wd)
    wspec = pl.BlockSpec((FCHUNK, D), lambda i: (i, 0))
    whole = lambda *shape: pl.BlockSpec(shape, lambda i: (0, 0))
    back, pg, pu, pd = pl.pallas_call(
        expert_kernel,
        name="expert",
        grid=(FF // FCHUNK,),
        out_shape=(sd((big, LANES), BF),) + (sd((FF, D), BF),) * 3,
        in_specs=[whole(big, LANES), whole(GROWS, GROWS)] + [wspec] * 3,
        out_specs=(whole(big, LANES),) + (wspec,) * 3,
        scratch_shapes=[pltpu.VMEM((SLOTS, D), BF)] * 2 + [pltpu.VMEM((SLOTS, D), F32)] * 2,
        compiler_params=pltpu.CompilerParams(vmem_limit_bytes=60 << 20),
    )(received.reshape(big, LANES), perm, fg, fu, fd)
    returned, gg, gu, gd = pl.pallas_call(
        return_kernel,
        name="giveback",
        out_shape=(sd((NEXP, PEER, LANES), BF),) + (sd((SH, D), BF),) * 3,
        in_specs=[anyw] * 4,
        out_specs=(anyw, vm, vm, vm),
        scratch_shapes=[
            reg((6,)),
            dma,
            dma,
            dma((10,)),
            pltpu.VMEM((2, 3, HALF, D), BF),
            pltpu.VMEM((2, 3, HALF, D), BF),
            pltpu.VMEM((2, 3, HALF, D), BF),
            pltpu.VMEM((2, 3, SH, D), BF),
            pltpu.VMEM((3, SH, D), BF),
            dma((6, 3)),
            dma((6, 3)),
        ],
        compiler_params=pltpu.CompilerParams(collective_id=2, has_side_effects=True, vmem_limit_bytes=48 << 20),
    )(back.reshape(NEXP, PEER, LANES), pg, pu, pd)
    output, d_tokens, d_scores = pl.pallas_call(
        combine_kernel,
        name="combine",
        out_shape=(sd((TOK, D), BF), sd((TOK, D), BF), sd((TOK, 2), F32)),
        in_specs=[vm] * 6,
        out_specs=(vm,) * 3,
        scratch_shapes=[pltpu.VMEM((SLOTS, D), BF)] * 2,
        compiler_params=pltpu.CompilerParams(vmem_limit_bytes=48 << 20),
    )(returned.reshape(big, LANES), perm, out_grad, expert_ids, ids_t, gate_scores)
    return output, d_tokens, d_scores, gg[None], gu[None], gd[None]


def solution(mesh):
    rows, weights = P(("expert", "dp"), None), P("expert", "dp", None)
    return jax.shard_map(
        shards,
        mesh=mesh,
        in_specs=(rows, rows, rows, weights, weights, weights, rows),
        out_specs=(rows, rows, rows, weights, weights, weights),
        check_vma=False,
    )
```

```python
import functools

import jax
import jax.numpy as jnp
import numpy as np
from jax import lax
from jax.experimental import pallas as pl
from jax.experimental.pallas import tpu as pltpu
from jax.sharding import PartitionSpec as P

MESH = pl.DeviceIdType.MESH
D, FF, TOK, CAP, NEXP, NDP = 2048, 768, 128, 6, 64, 4
SH = FF // NDP
HALF = SH // 2
SLOTS = NEXP * CAP
LANES = 512
PIECES = D // LANES
PEER = 2 * PIECES * CAP
GRP = 8
GROWS = GRP * PEER
GSLOTS = GRP * CAP
BF, F32, I32 = jnp.bfloat16, jnp.float32, jnp.int32
FCHUNK = 256

_r = np.arange(GROWS)
_peer, _kind, _piece, _slot = _r // PEER, _r % PEER // (PIECES * CAP), _r % (PIECES * CAP) // CAP, _r % CAP
_dest = (_kind * PIECES + _piece) * GSLOTS + _peer * CAP + _slot
PERM = np.zeros((GROWS, GROWS), np.float32)
PERM[_dest, _r] = 1.0


def dot(a, b, ca=1, cb=0):
    return lax.dot_general(a, b, (((ca,), (cb,)), ((), ())), preferred_element_type=F32)


def place():
    me, y = lax.axis_index("expert"), lax.axis_index("dp")
    return me, y, me // 8, (me // 2) % 4, me % 2


def tell(sem, devices):
    for d in devices:
        pl.semaphore_signal(sem, inc=1, device_id=d, device_id_type=MESH)


def barrier(sems, greeted=None, between=None):
    me, y, z, x, c = place()
    at = lambda z, x, c: z * 8 + x * 2 + c
    zs = [at((z + 1) % 8, x, c), at((z + 7) % 8, x, c)]
    xs = [at(z, (x + 1) % 4, c), at(z, (x + 3) % 4, c)]
    cs = [at(z, x, 1 - c)]
    bar = pltpu.get_barrier_semaphore()
    tell(bar, [(d, y) for d in zs + xs + cs] + [(me, (y + 1) % 4), (me, (y + 3) % 4)])
    pl.semaphore_wait(bar, 7)
    if greeted is not None:
        greeted()
    for i, group in enumerate((zs, zs, zs, xs, xs, cs)):
        tell(sems.at[i], [(d, y) for d in group])
        if between is not None:
            between(i)
        pl.semaphore_wait(sems.at[i], len(group))


def remote(src, dst, send, recv, device):
    return pltpu.make_async_remote_copy(src, dst, send, recv, device_id=device, device_id_type=MESH)


def start_exchange(src, dst, send, recv, local):
    me, y, z, x, c = place()
    own = pltpu.make_async_copy(src.at[me], dst.at[me], local)
    own.start()

    def one(k, carry):
        peer = ((z + k // 8) % 8) * 8 + ((x + (k // 2) % 4) % 4) * 2 + (c + k % 2) % 2
        remote(src.at[peer], dst.at[me], send, recv, (peer, y)).start()
        return carry

    lax.fori_loop(1, NEXP, one, 0)
    return own


def finish_exchange(src, dst, send, recv, own):
    n = NEXP - 1
    pltpu.make_async_copy(dst.at[pl.ds(0, n)], dst.at[pl.ds(0, n)], recv).wait()
    pltpu.make_async_copy(src.at[pl.ds(0, n)], src.at[pl.ds(0, n)], send).wait()
    own.wait()


def targets_row(ids, ids_t):
    before = lax.broadcasted_iota(I32, (TOK, TOK), 0) < lax.broadcasted_iota(I32, (TOK, TOK), 1)
    out = []
    for k in range(2):
        mine = ids_t[k : k + 1, :]
        same = (ids[:, 0:1] == mine).astype(F32) + (ids[:, 1:2] == mine).astype(F32)
        pos = jnp.sum(jnp.where(before, same, 0.0), axis=0, keepdims=True)
        out.append(mine * CAP + pos)
    return out


def targets_col(ids, ids_t):
    before = lax.broadcasted_iota(I32, (TOK, TOK), 1) < lax.broadcasted_iota(I32, (TOK, TOK), 0)
    out = []
    for k in range(2):
        mine = ids[:, k : k + 1]
        same = (ids_t[0:1, :] == mine).astype(F32) + (ids_t[1:2, :] == mine).astype(F32)
        pos = jnp.sum(jnp.where(before, same, 0.0), axis=1, keepdims=True)
        out.append(mine * CAP + pos)
    return out


def columns(pair):
    return jnp.concatenate([pair] * 4, axis=0).T


def pack_group(g, ids_t, ids, sc_t, out, table):
    t0, t1 = targets_row(ids, ids_t)
    s0, s1 = sc_t[0:1, :], sc_t[1:2, :]
    row = lax.broadcasted_iota(I32, (GROWS, 1), 0).astype(F32)
    six = jnp.floor((row + 0.5) * (1.0 / CAP))
    peer = jnp.floor((six + 0.5) * (1.0 / (2 * PIECES)))
    block = six - 2 * PIECES * peer
    slot = peer * CAP + (row - CAP * six) + float(g * GSLOTS)
    h0, h1 = t0 == slot, t1 == slot
    score = jnp.sum(jnp.where(h0, s0, 0.0) + jnp.where(h1, s1, 0.0), axis=1, keepdims=True)
    scale = jnp.where(block > PIECES - 0.5, score, 1.0)
    hit = h0.astype(F32) + h1.astype(F32)
    pick = jnp.concatenate([jnp.where(block == float(b), hit, 0.0).astype(BF) for b in range(2 * PIECES)], axis=1)
    rows = dot(pick, table[...]) * scale
    out[g * GRP : (g + 1) * GRP] = rows.astype(BF).reshape(GRP, PEER, LANES)


def dispatch_kernel(
    tok, grad, ids, sc, wg, wu, wd, out, fg, fu, fd, bsem, xs, xr, loc, ws, wr, tv, gv, iv, sv, table, x
):
    me, y, *_ = place()
    up, dn = (y + 1) % 4, (y + 3) % 4
    shards, fulls = (wg, wu, wd), (fg, fu, fd)
    at = lambda ref, who, off, n: ref.at[pl.ds(pl.multiple_of(who * SH + off, 32), n)]
    loads = [
        pltpu.make_async_copy(s, d, loc.at[4 + i]) for i, (s, d) in enumerate(((ids, iv), (sc, sv), (tok, tv), (grad, gv)))
    ]
    mine = [pltpu.make_async_copy(s, at(f, y, 0, SH), loc.at[1 + m]) for m, (s, f) in enumerate(zip(shards, fulls))]
    for q in loads + mine:
        q.start()
    first, relay = [], []

    def gather():
        for m, (s, f) in enumerate(zip(shards, fulls)):
            for way, to in enumerate((up, dn)):
                q = remote(s, at(f, y, 0, SH), ws.at[way, m], wr.at[way, m], (me, to))
                q.start()
                first.append((m, way, q))

    def pack(i):
        if i == 0:
            for q in loads:
                q.wait()
            for piece in range(PIECES):
                lanes = slice(piece * LANES, (piece + 1) * LANES)
                table[piece * TOK : (piece + 1) * TOK, :] = tv[:, lanes]
                table[(PIECES + piece) * TOK : (PIECES + piece + 1) * TOK, :] = gv[:, lanes]
        ids_t = iv[...].astype(F32)
        for g in ((0,), (1, 2), (3, 4), (5, 6), (7,), ())[i]:
            pack_group(g, ids_t, columns(ids_t), sv[...], x, table)

    barrier(bsem, gather, pack)
    own = start_exchange(x, out, xs, xr, loc.at[0])
    for m, way, q in first:
        q.wait_recv()
        part = at(fulls[m], dn if way == 0 else up, way * HALF, HALF)
        r = remote(part, part, ws.at[2 + way, m], wr.at[2 + way, m], (me, up if way == 0 else dn))
        r.start()
        relay.append(r)
    for q in relay:
        q.wait()
    for _, _, q in first:
        q.wait_send()
    for q in mine:
        q.wait()
    finish_exchange(x, out, xs, xr, own)


def unpack_rows(perm, rows, first, second, start=0, stop=NEXP // GRP):
    def one(g, carry):
        z = dot(perm[...], rows[pl.ds(pl.multiple_of(g * GROWS, GROWS), GROWS), :]).astype(BF)
        at = pl.ds(pl.multiple_of(g * GSLOTS, GSLOTS), GSLOTS)
        for kind, ref in enumerate((first, second)):
            for piece in range(PIECES):
                o = (kind * PIECES + piece) * GSLOTS
                ref[at, piece * LANES : (piece + 1) * LANES] = z[o : o + GSLOTS]
        return carry

    lax.fori_loop(start, stop, one, 0)


def pack_rows(perm, out, first, second):
    def one(g, carry):
        at = pl.ds(pl.multiple_of(g * GSLOTS, GSLOTS), GSLOTS)
        z = [
            ref[at, piece * LANES : (piece + 1) * LANES].astype(BF)
            for ref in (first, second)
            for piece in range(PIECES)
        ]
        packed = dot(perm[...], jnp.concatenate(z, axis=0), 0, 0)
        out[pl.ds(pl.multiple_of(g * GROWS, GROWS), GROWS), :] = packed.astype(BF)
        return carry

    lax.fori_loop(0, NEXP // GRP, one, 0)


def expert_kernel(rows, perm, wg, wu, wd, out, dg, du, dd, xt, xc, acc_o, acc_i):
    step = pl.program_id(0)

    @pl.when(step == 0)
    def _():
        unpack_rows(perm, rows, xt, xc)

    gate = dot(xt[...], wg[...], 1, 1)
    up = dot(xt[...], wu[...], 1, 1)
    hg = dot(xc[...], wd[...], 1, 1)
    s = jax.nn.sigmoid(gate)
    act = gate * s
    hidden = (act * up).astype(BF)
    ggrad = (hg * up * (s * (1.0 + gate * (1.0 - s)))).astype(BF)
    ugrad = (hg * act).astype(BF)
    dg[...] = dot(ggrad, xt[...], 0, 0).astype(BF)
    du[...] = dot(ugrad, xt[...], 0, 0).astype(BF)
    dd[...] = dot(hidden, xc[...], 0, 0).astype(BF)
    o = dot(hidden, wd[...])
    i = dot(ggrad, wg[...]) + dot(ugrad, wu[...])

    @pl.when(step == 0)
    def _():
        acc_o[...] = o
        acc_i[...] = i

    @pl.when(step > 0)
    def _():
        acc_o[...] += o
        acc_i[...] += i

    @pl.when(step == FF // FCHUNK - 1)
    def _():
        pack_rows(perm, out, acc_o, acc_i)


def return_kernel(
    x, pg, pu, pd, out, frm, bsem, xs, xr, loc, rel, add, summed, rs_s, rs_r
):
    me, y, *_ = place()
    up, dn, far = (y + 1) % 4, (y + 3) % 4, (y + 2) % 4
    parts = (pg, pu, pd)
    at = lambda ref, who, off, n: ref.at[pl.ds(pl.multiple_of(who * SH + off, 32), n)]
    loads = []
    for m, p in enumerate(parts):
        qs = [
            pltpu.make_async_copy(at(p, up, 0, HALF), add.at[0, m], loc.at[1 + m]),
            pltpu.make_async_copy(at(p, dn, HALF, HALF), add.at[1, m], loc.at[4 + m]),
        ]
        for q in qs:
            q.start()
        loads.append(qs)
    barrier(bsem)
    tos = (up, dn)
    relays, directs, sums = [], [], []
    for m, p in enumerate(parts):
        for way in range(2):
            q = remote(at(p, far, way * HALF, HALF), rel.at[way, m], rs_s.at[way, m], rs_r.at[way, m], (me, tos[way]))
            q.start()
            relays.append((m, way, q))
    for m, p in enumerate(parts):
        for way in range(2):
            off = (1 - way) * HALF
            q = remote(
                at(p, tos[way], off, HALF),
                frm.at[way, m, pl.ds(off, HALF)],
                rs_s.at[2 + way, m],
                rs_r.at[2 + way, m],
                (me, tos[way]),
            )
            q.start()
            directs.append(q)
    own = start_exchange(x, out, xs, xr, loc.at[0])
    for m, way, q in relays:
        q.wait_recv()
        loads[m][way].wait()

        def add_rows(r, carry):
            rows = pl.ds(pl.multiple_of(r * 32, 32), 32)
            total = rel[way, m, rows, :].astype(F32) + add[way, m, rows, :].astype(F32)
            summed[way, m, rows, :] = total.astype(BF)
            return carry

        lax.fori_loop(0, HALF // 32, add_rows, 0)
        off = way * HALF
        s = remote(
            summed.at[way, m], frm.at[way, m, pl.ds(off, HALF)], rs_s.at[4 + way, m], rs_r.at[4 + way, m], (me, tos[way])
        )
        s.start()
        sums.append(s)
    for q in directs:
        q.wait()
    for q in sums:
        q.wait()
    for _, _, q in relays:
        q.wait_send()
    finish_exchange(x, out, xs, xr, own)


def combine_kernel(
    rows_h, frm_h, perm_h, grad_h, ids_h, sc_h, pg, pu, pd,
    out, dtok, dsc, og, ou, od,
    rows, frm, perm, grad, ids, sc, xo, xi, own, fin, sem, rsem,
):
    y = lax.axis_index("dp")
    parts, outs = (pg, pu, pd), (og, ou, od)
    small = [
        pltpu.make_async_copy(s, d, sem.at[6 + i])
        for i, (s, d) in enumerate(((perm_h, perm), (grad_h, grad), (ids_h, ids), (sc_h, sc)))
    ]
    span = 2 * GROWS
    chunks = [
        pltpu.make_async_copy(rows_h.at[pl.ds(i * span, span)], rows.at[pl.ds(i * span, span)], rsem.at[i]) for i in range(4)
    ]
    load = [
        [
            pltpu.make_async_copy(p.at[pl.ds(pl.multiple_of(y * SH, 32), SH)], own.at[m], sem.at[m]),
            pltpu.make_async_copy(frm_h.at[0, m], frm.at[0, m], sem.at[10 + m]),
            pltpu.make_async_copy(frm_h.at[1, m], frm.at[1, m], sem.at[13 + m]),
        ]
        for m, p in enumerate(parts)
    ]
    store = [pltpu.make_async_copy(fin.at[m], o, sem.at[3 + m]) for m, o in enumerate(outs)]
    for q in small + chunks + sum(load, []):
        q.start()
    for q in small:
        q.wait()
    for i in range(4):
        chunks[i].wait()
        unpack_rows(perm, rows, xo, xi, 2 * i, 2 * i + 2)
    for m in range(3):
        for q in load[m]:
            q.wait()

        def final(r, carry):
            at = pl.ds(pl.multiple_of(r * 32, 32), 32)
            total = own[m, at, :].astype(F32) + frm[0, m, at, :].astype(F32)
            fin[m, at, :] = (total + frm[1, m, at, :].astype(F32)).astype(BF)
            return carry

        lax.fori_loop(0, SH // 32, final, 0)
        store[m].start()
    ids_t = ids[...].astype(F32)
    t0, t1 = targets_col(columns(ids_t), ids_t)
    slot = lax.broadcasted_iota(I32, (TOK, SLOTS), 1).astype(F32)
    g0 = (t0 == slot).astype(F32).astype(BF)
    g1 = (t1 == slot).astype(F32).astype(BF)
    both = g0 + g1
    sc_c = columns(sc[...])
    s0, s1 = sc_c[:, 0:1], sc_c[:, 1:2]
    d0 = jnp.zeros((TOK, 1), F32)
    d1 = jnp.zeros((TOK, 1), F32)
    for piece in range(PIECES):
        lanes = slice(piece * LANES, (piece + 1) * LANES)
        p0 = dot(g0, xo[:, lanes])
        p1 = dot(g1, xo[:, lanes])
        cot = grad[:, lanes].astype(F32)
        out[:, lanes] = (s0 * p0 + s1 * p1).astype(BF)
        d0 += jnp.sum(cot * p0, axis=1, keepdims=True)
        d1 += jnp.sum(cot * p1, axis=1, keepdims=True)
        dtok[:, lanes] = dot(both, xi[:, lanes]).astype(BF)
    dsc[...] = jnp.concatenate([d0, d1] * 4, axis=1).T[0:2, :]
    for q in store:
        q.wait()


def shards(tokens, expert_ids, gate_scores, gate_proj, up_proj, down_proj, out_grad):
    sd = jax.ShapeDtypeStruct
    vm = pl.BlockSpec(memory_space=pltpu.VMEM)
    anyw = pl.BlockSpec(memory_space=pl.ANY)
    dma, reg = pltpu.SemaphoreType.DMA, pltpu.SemaphoreType.REGULAR
    ids_t, sc_t = expert_ids.T, gate_scores.T
    perm = jnp.asarray(PERM, BF)
    big = NEXP * PEER
    wg, wu, wd = gate_proj[0], up_proj[0], down_proj[0]
    received, fg, fu, fd = pl.pallas_call(
        dispatch_kernel,
        name="dispatch",
        out_shape=(sd((NEXP, PEER, LANES), BF),) + (sd((FF, D), BF),) * 3,
        in_specs=[anyw] * 7,
        out_specs=(anyw,) * 4,
        scratch_shapes=[
            reg((6,)),
            dma,
            dma,
            dma((8,)),
            dma((4, 3)),
            dma((4, 3)),
            pltpu.VMEM((TOK, D), BF),
            pltpu.VMEM((TOK, D), BF),
            pltpu.VMEM((2, TOK), I32),
            pltpu.VMEM((2, TOK), F32),
            pltpu.VMEM((2 * PIECES * TOK, LANES), BF),
            pltpu.VMEM((NEXP, PEER, LANES), BF),
        ],
        compiler_params=pltpu.CompilerParams(collective_id=1, has_side_effects=True, vmem_limit_bytes=62 << 20),
    )(tokens, out_grad, ids_t, sc_t, wg, wu, wd)
    wspec = pl.BlockSpec((FCHUNK, D), lambda i: (i, 0))
    whole = lambda *shape: pl.BlockSpec(shape, lambda i: (0, 0))
    back, pg, pu, pd = pl.pallas_call(
        expert_kernel,
        name="expert",
        grid=(FF // FCHUNK,),
        out_shape=(sd((big, LANES), BF),) + (sd((FF, D), BF),) * 3,
        in_specs=[whole(big, LANES), whole(GROWS, GROWS)] + [wspec] * 3,
        out_specs=(whole(big, LANES),) + (wspec,) * 3,
        scratch_shapes=[pltpu.VMEM((SLOTS, D), BF)] * 2 + [pltpu.VMEM((SLOTS, D), F32)] * 2,
        compiler_params=pltpu.CompilerParams(vmem_limit_bytes=60 << 20),
    )(received.reshape(big, LANES), perm, fg, fu, fd)
    returned, frm = pl.pallas_call(
        return_kernel,
        name="giveback",
        out_shape=(sd((NEXP, PEER, LANES), BF), sd((2, 3, SH, D), BF)),
        in_specs=[anyw] * 4,
        out_specs=(anyw, anyw),
        scratch_shapes=[
            reg((6,)),
            dma,
            dma,
            dma((7,)),
            pltpu.VMEM((2, 3, HALF, D), BF),
            pltpu.VMEM((2, 3, HALF, D), BF),
            pltpu.VMEM((2, 3, HALF, D), BF),
            dma((6, 3)),
            dma((6, 3)),
        ],
        compiler_params=pltpu.CompilerParams(collective_id=2, has_side_effects=True, vmem_limit_bytes=62 << 20),
    )(back.reshape(NEXP, PEER, LANES), pg, pu, pd)
    output, d_tokens, d_scores_t, gg, gu, gd = pl.pallas_call(
        combine_kernel,
        name="combine",
        out_shape=(sd((TOK, D), BF), sd((TOK, D), BF), sd((2, TOK), F32)) + (sd((SH, D), BF),) * 3,
        in_specs=[anyw] * 9,
        out_specs=(vm,) * 3 + (anyw,) * 3,
        scratch_shapes=[
            pltpu.VMEM((big, LANES), BF),
            pltpu.VMEM((2, 3, SH, D), BF),
            pltpu.VMEM((GROWS, GROWS), BF),
            pltpu.VMEM((TOK, D), BF),
            pltpu.VMEM((2, TOK), I32),
            pltpu.VMEM((2, TOK), F32),
        ]
        + [pltpu.VMEM((SLOTS, D), BF)] * 2
        + [pltpu.VMEM((3, SH, D), BF)] * 2
        + [dma((16,)), dma((4,))],
        compiler_params=pltpu.CompilerParams(vmem_limit_bytes=62 << 20),
    )(returned.reshape(big, LANES), frm, perm, out_grad, ids_t, sc_t, pg, pu, pd)
    d_scores = d_scores_t.T
    return output, d_tokens, d_scores, gg[None], gu[None], gd[None]


def solution(mesh):
    rows, weights = P(("expert", "dp"), None), P("expert", "dp", None)
    return jax.shard_map(
        shards,
        mesh=mesh,
        in_specs=(rows, rows, rows, weights, weights, weights, rows),
        out_specs=(rows, rows, rows, weights, weights, weights),
        check_vma=False,
    )
```

```python
import functools

import jax
import jax.numpy as jnp
import numpy as np
from jax import lax
from jax.experimental import pallas as pl
from jax.experimental.pallas import tpu as pltpu
from jax.sharding import PartitionSpec as P

MESH = pl.DeviceIdType.MESH
D, FF, TOK, CAP, NEXP, NDP = 2048, 768, 128, 6, 64, 4
SH = FF // NDP
HALF = SH // 2
SLOTS = NEXP * CAP
LANES = 512
PIECES = D // LANES
PEER = 2 * PIECES * CAP
GRP = 8
GROWS = GRP * PEER
GSLOTS = GRP * CAP
BF, F32, I32 = jnp.bfloat16, jnp.float32, jnp.int32
FCHUNK = 256

_r = np.arange(GROWS)
_peer, _kind, _piece, _slot = _r // PEER, _r % PEER // (PIECES * CAP), _r % (PIECES * CAP) // CAP, _r % CAP
_dest = (_kind * PIECES + _piece) * GSLOTS + _peer * CAP + _slot
PERM = np.zeros((GROWS, GROWS), np.float32)
PERM[_dest, _r] = 1.0


def dot(a, b, ca=1, cb=0):
    return lax.dot_general(a, b, (((ca,), (cb,)), ((), ())), preferred_element_type=F32)


def place():
    me, y = lax.axis_index("expert"), lax.axis_index("dp")
    return me, y, me // 8, (me // 2) % 4, me % 2


def tell(sem, devices):
    for d in devices:
        pl.semaphore_signal(sem, inc=1, device_id=d, device_id_type=MESH)


def barrier(sems, greeted=None, between=None):
    me, y, z, x, c = place()
    at = lambda z, x, c: z * 8 + x * 2 + c
    zs = [at((z + 1) % 8, x, c), at((z + 7) % 8, x, c)]
    xs = [at(z, (x + 1) % 4, c), at(z, (x + 3) % 4, c)]
    cs = [at(z, x, 1 - c)]
    bar = pltpu.get_barrier_semaphore()
    tell(bar, [(d, y) for d in zs + xs + cs] + [(me, (y + 1) % 4), (me, (y + 3) % 4)])
    pl.semaphore_wait(bar, 7)
    if greeted is not None:
        greeted()
    for i, group in enumerate((zs, zs, zs, xs, xs, cs)):
        tell(sems.at[i], [(d, y) for d in group])
        if between is not None:
            between(i)
        pl.semaphore_wait(sems.at[i], len(group))


def remote(src, dst, send, recv, device):
    return pltpu.make_async_remote_copy(src, dst, send, recv, device_id=device, device_id_type=MESH)


def start_exchange(src, dst, send, recv, local):
    me, y, z, x, c = place()
    own = pltpu.make_async_copy(src.at[me], dst.at[me], local)
    own.start()

    def one(k, carry):
        peer = ((z + k // 8) % 8) * 8 + ((x + (k // 2) % 4) % 4) * 2 + (c + k % 2) % 2
        remote(src.at[peer], dst.at[me], send, recv, (peer, y)).start()
        return carry

    lax.fori_loop(1, NEXP, one, 0)
    return own


def finish_exchange(src, dst, send, recv, own):
    n = NEXP - 1
    pltpu.make_async_copy(dst.at[pl.ds(0, n)], dst.at[pl.ds(0, n)], recv).wait()
    pltpu.make_async_copy(src.at[pl.ds(0, n)], src.at[pl.ds(0, n)], send).wait()
    own.wait()


def targets_row(ids, ids_t):
    before = lax.broadcasted_iota(I32, (TOK, TOK), 0) < lax.broadcasted_iota(I32, (TOK, TOK), 1)
    out = []
    for k in range(2):
        mine = ids_t[k : k + 1, :]
        same = (ids[:, 0:1] == mine).astype(F32) + (ids[:, 1:2] == mine).astype(F32)
        pos = jnp.sum(jnp.where(before, same, 0.0), axis=0, keepdims=True)
        out.append(mine * CAP + pos)
    return out


def targets_col(ids, ids_t):
    before = lax.broadcasted_iota(I32, (TOK, TOK), 1) < lax.broadcasted_iota(I32, (TOK, TOK), 0)
    out = []
    for k in range(2):
        mine = ids[:, k : k + 1]
        same = (ids_t[0:1, :] == mine).astype(F32) + (ids_t[1:2, :] == mine).astype(F32)
        pos = jnp.sum(jnp.where(before, same, 0.0), axis=1, keepdims=True)
        out.append(mine * CAP + pos)
    return out


def columns(pair):
    return jnp.concatenate([pair] * 4, axis=0).T


def pack_group(g, ids_t, ids, sc_t, out, table):
    t0, t1 = targets_row(ids, ids_t)
    s0, s1 = sc_t[0:1, :], sc_t[1:2, :]
    row = lax.broadcasted_iota(I32, (GROWS, 1), 0).astype(F32)
    six = jnp.floor((row + 0.5) * (1.0 / CAP))
    peer = jnp.floor((six + 0.5) * (1.0 / (2 * PIECES)))
    block = six - 2 * PIECES * peer
    slot = peer * CAP + (row - CAP * six) + float(g * GSLOTS)
    h0, h1 = t0 == slot, t1 == slot
    score = jnp.sum(jnp.where(h0, s0, 0.0) + jnp.where(h1, s1, 0.0), axis=1, keepdims=True)
    scale = jnp.where(block > PIECES - 0.5, score, 1.0)
    hit = h0.astype(F32) + h1.astype(F32)
    pick = jnp.concatenate([jnp.where(block == float(b), hit, 0.0).astype(BF) for b in range(2 * PIECES)], axis=1)
    rows = dot(pick, table[...]) * scale
    out[g * GRP : (g + 1) * GRP] = rows.astype(BF).reshape(GRP, PEER, LANES)


def dispatch_kernel(
    tok, grad, ids, sc, wg, wu, wd, out, fg, fu, fd, bsem, xs, xr, loc, ws, wr, tv, gv, iv, sv, table, x
):
    me, y, *_ = place()
    up, dn = (y + 1) % 4, (y + 3) % 4
    shards, fulls = (wg, wu, wd), (fg, fu, fd)
    at = lambda ref, who, off, n: ref.at[pl.ds(pl.multiple_of(who * SH + off, 32), n)]
    loads = [
        pltpu.make_async_copy(s, d, loc.at[4 + i]) for i, (s, d) in enumerate(((ids, iv), (sc, sv), (tok, tv), (grad, gv)))
    ]
    mine = [pltpu.make_async_copy(s, at(f, y, 0, SH), loc.at[1 + m]) for m, (s, f) in enumerate(zip(shards, fulls))]
    for q in loads + mine:
        q.start()
    first, relay = [], []

    def gather():
        for m, (s, f) in enumerate(zip(shards, fulls)):
            for way, to in enumerate((up, dn)):
                q = remote(s, at(f, y, 0, SH), ws.at[way, m], wr.at[way, m], (me, to))
                q.start()
                first.append((m, way, q))

    def pack(i):
        if i == 0:
            for q in loads:
                q.wait()
            for piece in range(PIECES):
                lanes = slice(piece * LANES, (piece + 1) * LANES)
                table[piece * TOK : (piece + 1) * TOK, :] = tv[:, lanes]
                table[(PIECES + piece) * TOK : (PIECES + piece + 1) * TOK, :] = gv[:, lanes]
        ids_t = iv[...].astype(F32)
        for g in ((0,), (1, 2), (3, 4), (5, 6), (7,), ())[i]:
            pack_group(g, ids_t, columns(ids_t), sv[...], x, table)

    barrier(bsem, gather, pack)
    own = start_exchange(x, out, xs, xr, loc.at[0])
    for m, way, q in first:
        q.wait_recv()
        part = at(fulls[m], dn if way == 0 else up, way * HALF, HALF)
        r = remote(part, part, ws.at[2 + way, m], wr.at[2 + way, m], (me, up if way == 0 else dn))
        r.start()
        relay.append(r)
    for q in relay:
        q.wait()
    for _, _, q in first:
        q.wait_send()
    for q in mine:
        q.wait()
    finish_exchange(x, out, xs, xr, own)


def unpack_rows(perm, rows, first, second, start=0, stop=NEXP // GRP):
    def one(g, carry):
        z = dot(perm[...], rows[pl.ds(pl.multiple_of(g * GROWS, GROWS), GROWS), :]).astype(BF)
        at = pl.ds(pl.multiple_of(g * GSLOTS, GSLOTS), GSLOTS)
        for kind, ref in enumerate((first, second)):
            for piece in range(PIECES):
                o = (kind * PIECES + piece) * GSLOTS
                ref[at, piece * LANES : (piece + 1) * LANES] = z[o : o + GSLOTS]
        return carry

    lax.fori_loop(start, stop, one, 0)


def pack_rows(perm, out, first, second, start, stop):
    def one(g, carry):
        at = pl.ds(pl.multiple_of(g * GSLOTS, GSLOTS), GSLOTS)
        z = [ref[at, piece * LANES : (piece + 1) * LANES] for ref in (first, second) for piece in range(PIECES)]
        packed = dot(perm[...], jnp.concatenate(z, axis=0), 0, 0)
        out[pl.ds(g * GRP, GRP)] = packed.astype(BF).reshape(GRP, PEER, LANES)
        return carry

    lax.fori_loop(start, stop, one, 0)


def expert_kernel(rows, perm, wg, wu, wd, hid, gg, ug, dg, du, dd, xt, xc):
    @pl.when(pl.program_id(0) == 0)
    def _():
        unpack_rows(perm, rows, xt, xc)

    gate = dot(xt[...], wg[...], 1, 1)
    up = dot(xt[...], wu[...], 1, 1)
    hg = dot(xc[...], wd[...], 1, 1)
    s = jax.nn.sigmoid(gate)
    act = gate * s
    hidden = (act * up).astype(BF)
    ggrad = (hg * up * (s * (1.0 + gate * (1.0 - s)))).astype(BF)
    ugrad = (hg * act).astype(BF)
    hid[...], gg[...], ug[...] = hidden, ggrad, ugrad
    dg[...] = dot(ggrad, xt[...], 0, 0).astype(BF)
    du[...] = dot(ugrad, xt[...], 0, 0).astype(BF)
    dd[...] = dot(hidden, xc[...], 0, 0).astype(BF)


def return_kernel(
    hid_h, gg_h, ug_h, wd_h, wg_h, wu_h, perm_h, pg, pu, pd,
    out, frm,
    bsem, xs, xr, loc, csem, rel, add, summed, rs_s, rs_r,
    hid, gg, ug, wd, wg, wu, perm, xo, xi, x,
):
    me, y, *_ = place()
    up, dn, far = (y + 1) % 4, (y + 3) % 4, (y + 2) % 4
    parts = (pg, pu, pd)
    at = lambda ref, who, off, n: ref.at[pl.ds(pl.multiple_of(who * SH + off, 32), n)]
    lanes = [slice(piece * LANES, (piece + 1) * LANES) for piece in range(PIECES)]
    acts = [
        pltpu.make_async_copy(s, d, csem.at[i])
        for i, (s, d) in enumerate(((hid_h, hid), (gg_h, gg), (ug_h, ug), (perm_h, perm)))
    ]
    weights = [
        [
            pltpu.make_async_copy(s.at[:, cols], d.at[:, cols], csem.at[4 + 3 * piece + i])
            for i, (s, d) in enumerate(((wd_h, wd), (wg_h, wg), (wu_h, wu)))
        ]
        for piece, cols in enumerate(lanes)
    ]
    loads = [
        [
            pltpu.make_async_copy(at(p, up, 0, HALF), add.at[0, m], loc.at[1 + m]),
            pltpu.make_async_copy(at(p, dn, HALF, HALF), add.at[1, m], loc.at[4 + m]),
        ]
        for m, p in enumerate(parts)
    ]
    for q in acts + sum(weights, []) + sum(loads, []):
        q.start()
    tos = (up, dn)
    relays, directs, sums = [], [], []

    def scatter():
        for m, p in enumerate(parts):
            for way in range(2):
                q = remote(
                    at(p, far, way * HALF, HALF), rel.at[way, m], rs_s.at[way, m], rs_r.at[way, m], (me, tos[way])
                )
                q.start()
                relays.append((m, way, q))
        for m, p in enumerate(parts):
            for way in range(2):
                off = (1 - way) * HALF
                q = remote(
                    at(p, tos[way], off, HALF),
                    frm.at[way, m, pl.ds(off, HALF)],
                    rs_s.at[2 + way, m],
                    rs_r.at[2 + way, m],
                    (me, tos[way]),
                )
                q.start()
                directs.append(q)

    def compute(i):
        if i == 0:
            for q in acts:
                q.wait()
        if i < PIECES:
            for q in weights[i]:
                q.wait()
            cols = lanes[i]
            xo[:, cols] = dot(hid[...], wd[:, cols]).astype(BF)
            xi[:, cols] = (dot(gg[...], wg[:, cols]) + dot(ug[...], wu[:, cols])).astype(BF)
        else:
            half = NEXP // GRP // 2
            pack_rows(perm, x, xo, xi, (i - PIECES) * half, (i - PIECES + 1) * half)

    barrier(bsem, scatter, compute)
    own = start_exchange(x, out, xs, xr, loc.at[0])
    for m, way, q in relays:
        q.wait_recv()
        loads[m][way].wait()

        def add_rows(r, carry):
            rows = pl.ds(pl.multiple_of(r * 32, 32), 32)
            total = rel[way, m, rows, :].astype(F32) + add[way, m, rows, :].astype(F32)
            summed[way, m, rows, :] = total.astype(BF)
            return carry

        lax.fori_loop(0, HALF // 32, add_rows, 0)
        off = way * HALF
        s = remote(
            summed.at[way, m], frm.at[way, m, pl.ds(off, HALF)], rs_s.at[4 + way, m], rs_r.at[4 + way, m], (me, tos[way])
        )
        s.start()
        sums.append(s)
    for q in directs:
        q.wait()
    for q in sums:
        q.wait()
    for _, _, q in relays:
        q.wait_send()
    finish_exchange(x, out, xs, xr, own)


def combine_kernel(
    rows_h, frm_h, perm_h, grad_h, ids_h, sc_h, pg, pu, pd,
    out, dtok, dsc, og, ou, od,
    rows, frm, perm, grad, ids, sc, xo, xi, own, fin, sem, rsem,
):
    y = lax.axis_index("dp")
    parts, outs = (pg, pu, pd), (og, ou, od)
    small = [
        pltpu.make_async_copy(s, d, sem.at[6 + i])
        for i, (s, d) in enumerate(((perm_h, perm), (grad_h, grad), (ids_h, ids), (sc_h, sc)))
    ]
    span = 2 * GROWS
    chunks = [
        pltpu.make_async_copy(rows_h.at[pl.ds(i * span, span)], rows.at[pl.ds(i * span, span)], rsem.at[i]) for i in range(4)
    ]
    load = [
        [
            pltpu.make_async_copy(p.at[pl.ds(pl.multiple_of(y * SH, 32), SH)], own.at[m], sem.at[m]),
            pltpu.make_async_copy(frm_h.at[0, m], frm.at[0, m], sem.at[10 + m]),
            pltpu.make_async_copy(frm_h.at[1, m], frm.at[1, m], sem.at[13 + m]),
        ]
        for m, p in enumerate(parts)
    ]
    store = [pltpu.make_async_copy(fin.at[m], o, sem.at[3 + m]) for m, o in enumerate(outs)]
    for q in small + chunks + sum(load, []):
        q.start()
    for q in small:
        q.wait()
    for i in range(4):
        chunks[i].wait()
        unpack_rows(perm, rows, xo, xi, 2 * i, 2 * i + 2)
    for m in range(3):
        for q in load[m]:
            q.wait()

        def final(r, carry):
            at = pl.ds(pl.multiple_of(r * 32, 32), 32)
            total = own[m, at, :].astype(F32) + frm[0, m, at, :].astype(F32)
            fin[m, at, :] = (total + frm[1, m, at, :].astype(F32)).astype(BF)
            return carry

        lax.fori_loop(0, SH // 32, final, 0)
        store[m].start()
    ids_t = ids[...].astype(F32)
    t0, t1 = targets_col(columns(ids_t), ids_t)
    slot = lax.broadcasted_iota(I32, (TOK, SLOTS), 1).astype(F32)
    g0 = (t0 == slot).astype(F32).astype(BF)
    g1 = (t1 == slot).astype(F32).astype(BF)
    both = g0 + g1
    sc_c = columns(sc[...])
    s0, s1 = sc_c[:, 0:1], sc_c[:, 1:2]
    d0 = jnp.zeros((TOK, 1), F32)
    d1 = jnp.zeros((TOK, 1), F32)
    for piece in range(PIECES):
        lanes = slice(piece * LANES, (piece + 1) * LANES)
        p0 = dot(g0, xo[:, lanes])
        p1 = dot(g1, xo[:, lanes])
        cot = grad[:, lanes].astype(F32)
        out[:, lanes] = (s0 * p0 + s1 * p1).astype(BF)
        d0 += jnp.sum(cot * p0, axis=1, keepdims=True)
        d1 += jnp.sum(cot * p1, axis=1, keepdims=True)
        dtok[:, lanes] = dot(both, xi[:, lanes]).astype(BF)
    dsc[...] = jnp.concatenate([d0, d1] * 4, axis=1).T[0:2, :]
    for q in store:
        q.wait()


def shards(tokens, expert_ids, gate_scores, gate_proj, up_proj, down_proj, out_grad):
    sd = jax.ShapeDtypeStruct
    vm = pl.BlockSpec(memory_space=pltpu.VMEM)
    anyw = pl.BlockSpec(memory_space=pl.ANY)
    dma, reg = pltpu.SemaphoreType.DMA, pltpu.SemaphoreType.REGULAR
    ids_t, sc_t = expert_ids.T, gate_scores.T
    perm = jnp.asarray(PERM, BF)
    big = NEXP * PEER
    wg, wu, wd = gate_proj[0], up_proj[0], down_proj[0]
    received, fg, fu, fd = pl.pallas_call(
        dispatch_kernel,
        name="dispatch",
        out_shape=(sd((NEXP, PEER, LANES), BF),) + (sd((FF, D), BF),) * 3,
        in_specs=[anyw] * 7,
        out_specs=(anyw,) * 4,
        scratch_shapes=[
            reg((6,)),
            dma,
            dma,
            dma((8,)),
            dma((4, 3)),
            dma((4, 3)),
            pltpu.VMEM((TOK, D), BF),
            pltpu.VMEM((TOK, D), BF),
            pltpu.VMEM((2, TOK), I32),
            pltpu.VMEM((2, TOK), F32),
            pltpu.VMEM((2 * PIECES * TOK, LANES), BF),
            pltpu.VMEM((NEXP, PEER, LANES), BF),
        ],
        compiler_params=pltpu.CompilerParams(collective_id=1, has_side_effects=True, vmem_limit_bytes=62 << 20),
    )(tokens, out_grad, ids_t, sc_t, wg, wu, wd)
    wspec = pl.BlockSpec((FCHUNK, D), lambda i: (i, 0))
    hspec = pl.BlockSpec((SLOTS, FCHUNK), lambda i: (0, i))
    whole = lambda *shape: pl.BlockSpec(shape, lambda i: (0, 0))
    hid, ggrad, ugrad, pg, pu, pd = pl.pallas_call(
        expert_kernel,
        name="expert",
        grid=(FF // FCHUNK,),
        out_shape=(sd((SLOTS, FF), BF),) * 3 + (sd((FF, D), BF),) * 3,
        in_specs=[whole(big, LANES), whole(GROWS, GROWS)] + [wspec] * 3,
        out_specs=(hspec,) * 3 + (wspec,) * 3,
        scratch_shapes=[pltpu.VMEM((SLOTS, D), BF)] * 2,
        compiler_params=pltpu.CompilerParams(vmem_limit_bytes=62 << 20),
    )(received.reshape(big, LANES), perm, fg, fu, fd)
    returned, frm = pl.pallas_call(
        return_kernel,
        name="giveback",
        out_shape=(sd((NEXP, PEER, LANES), BF), sd((2, 3, SH, D), BF)),
        in_specs=[anyw] * 10,
        out_specs=(anyw, anyw),
        scratch_shapes=[reg((6,)), dma, dma, dma((7,)), dma((16,))]
        + [pltpu.VMEM((2, 3, HALF, D), BF)] * 3
        + [dma((6, 3)), dma((6, 3))]
        + [pltpu.VMEM((SLOTS, FF), BF)] * 3
        + [pltpu.VMEM((FF, D), BF)] * 3
        + [pltpu.VMEM((GROWS, GROWS), BF)]
        + [pltpu.VMEM((SLOTS, D), BF)] * 2
        + [pltpu.VMEM((NEXP, PEER, LANES), BF)],
        compiler_params=pltpu.CompilerParams(collective_id=2, has_side_effects=True, vmem_limit_bytes=62 << 20),
    )(hid, ggrad, ugrad, fd, fg, fu, perm, pg, pu, pd)
    output, d_tokens, d_scores_t, gg, gu, gd = pl.pallas_call(
        combine_kernel,
        name="combine",
        out_shape=(sd((TOK, D), BF), sd((TOK, D), BF), sd((2, TOK), F32)) + (sd((SH, D), BF),) * 3,
        in_specs=[anyw] * 9,
        out_specs=(vm,) * 3 + (anyw,) * 3,
        scratch_shapes=[
            pltpu.VMEM((big, LANES), BF),
            pltpu.VMEM((2, 3, SH, D), BF),
            pltpu.VMEM((GROWS, GROWS), BF),
            pltpu.VMEM((TOK, D), BF),
            pltpu.VMEM((2, TOK), I32),
            pltpu.VMEM((2, TOK), F32),
        ]
        + [pltpu.VMEM((SLOTS, D), BF)] * 2
        + [pltpu.VMEM((3, SH, D), BF)] * 2
        + [dma((16,)), dma((4,))],
        compiler_params=pltpu.CompilerParams(vmem_limit_bytes=62 << 20),
    )(returned.reshape(big, LANES), frm, perm, out_grad, ids_t, sc_t, pg, pu, pd)
    d_scores = d_scores_t.T
    return output, d_tokens, d_scores, gg[None], gu[None], gd[None]


def solution(mesh):
    rows, weights = P(("expert", "dp"), None), P("expert", "dp", None)
    return jax.shard_map(
        shards,
        mesh=mesh,
        in_specs=(rows, rows, rows, weights, weights, weights, rows),
        out_specs=(rows, rows, rows, weights, weights, weights),
        check_vma=False,
    )
```

```python
import functools

import jax
import jax.numpy as jnp
import numpy as np
from jax import lax
from jax.experimental import pallas as pl
from jax.experimental.pallas import tpu as pltpu
from jax.sharding import PartitionSpec as P

MESH = pl.DeviceIdType.MESH
D, FF, TOK, CAP, NEXP, NDP = 2048, 768, 128, 6, 64, 4
SH = FF // NDP
HALF = SH // 2
SLOTS = NEXP * CAP
LANES = 512
PIECES = D // LANES
PEER = 2 * PIECES * CAP
GRP = 8
GROWS = GRP * PEER
GSLOTS = GRP * CAP
BF, F32, I32 = jnp.bfloat16, jnp.float32, jnp.int32
FCHUNK = 256

_r = np.arange(GROWS)
_peer, _kind, _piece, _slot = _r // PEER, _r % PEER // (PIECES * CAP), _r % (PIECES * CAP) // CAP, _r % CAP
_dest = (_kind * PIECES + _piece) * GSLOTS + _peer * CAP + _slot
PERM = np.zeros((GROWS, GROWS), np.float32)
PERM[_dest, _r] = 1.0


def dot(a, b, ca=1, cb=0):
    return lax.dot_general(a, b, (((ca,), (cb,)), ((), ())), preferred_element_type=F32)


def place():
    me, y = lax.axis_index("expert"), lax.axis_index("dp")
    return me, y, me // 8, (me // 2) % 4, me % 2


def tell(sem, devices):
    for d in devices:
        pl.semaphore_signal(sem, inc=1, device_id=d, device_id_type=MESH)


def barrier(sems, greeted=None, between=None):
    me, y, z, x, c = place()
    at = lambda z, x, c: z * 8 + x * 2 + c
    zs = [at((z + 1) % 8, x, c), at((z + 7) % 8, x, c)]
    xs = [at(z, (x + 1) % 4, c), at(z, (x + 3) % 4, c)]
    cs = [at(z, x, 1 - c)]
    bar = pltpu.get_barrier_semaphore()
    tell(bar, [(d, y) for d in zs + xs + cs] + [(me, (y + 1) % 4), (me, (y + 3) % 4)])
    pl.semaphore_wait(bar, 7)
    if greeted is not None:
        greeted()
    for i, group in enumerate((zs, zs, zs, xs, xs, cs)):
        tell(sems.at[i], [(d, y) for d in group])
        if between is not None:
            between(i)
        pl.semaphore_wait(sems.at[i], len(group))


def remote(src, dst, send, recv, device):
    return pltpu.make_async_remote_copy(src, dst, send, recv, device_id=device, device_id_type=MESH)


def start_exchange(src, dst, send, recv, local):
    me, y, z, x, c = place()
    own = pltpu.make_async_copy(src.at[me], dst.at[me], local)
    own.start()

    def one(k, carry):
        peer = ((z + k // 8) % 8) * 8 + ((x + (k // 2) % 4) % 4) * 2 + (c + k % 2) % 2
        remote(src.at[peer], dst.at[me], send, recv, (peer, y)).start()
        return carry

    lax.fori_loop(1, NEXP, one, 0)
    return own


def finish_exchange(src, dst, send, recv, own):
    n = NEXP - 1
    pltpu.make_async_copy(dst.at[pl.ds(0, n)], dst.at[pl.ds(0, n)], recv).wait()
    pltpu.make_async_copy(src.at[pl.ds(0, n)], src.at[pl.ds(0, n)], send).wait()
    own.wait()


def targets_row(ids, ids_t):
    before = lax.broadcasted_iota(I32, (TOK, TOK), 0) < lax.broadcasted_iota(I32, (TOK, TOK), 1)
    out = []
    for k in range(2):
        mine = ids_t[k : k + 1, :]
        same = (ids[:, 0:1] == mine).astype(F32) + (ids[:, 1:2] == mine).astype(F32)
        pos = jnp.sum(jnp.where(before, same, 0.0), axis=0, keepdims=True)
        out.append(mine * CAP + pos)
    return out


def targets_col(ids, ids_t):
    before = lax.broadcasted_iota(I32, (TOK, TOK), 1) < lax.broadcasted_iota(I32, (TOK, TOK), 0)
    out = []
    for k in range(2):
        mine = ids[:, k : k + 1]
        same = (ids_t[0:1, :] == mine).astype(F32) + (ids_t[1:2, :] == mine).astype(F32)
        pos = jnp.sum(jnp.where(before, same, 0.0), axis=1, keepdims=True)
        out.append(mine * CAP + pos)
    return out


def columns(pair):
    return jnp.concatenate([pair] * 4, axis=0).T


def pack_group(g, ids_t, ids, sc_t, out, table):
    t0, t1 = targets_row(ids, ids_t)
    s0, s1 = sc_t[0:1, :], sc_t[1:2, :]
    row = lax.broadcasted_iota(I32, (GROWS, 1), 0).astype(F32)
    six = jnp.floor((row + 0.5) * (1.0 / CAP))
    peer = jnp.floor((six + 0.5) * (1.0 / (2 * PIECES)))
    block = six - 2 * PIECES * peer
    slot = peer * CAP + (row - CAP * six) + float(g * GSLOTS)
    h0, h1 = t0 == slot, t1 == slot
    score = jnp.sum(jnp.where(h0, s0, 0.0) + jnp.where(h1, s1, 0.0), axis=1, keepdims=True)
    scale = jnp.where(block > PIECES - 0.5, score, 1.0)
    hit = h0.astype(F32) + h1.astype(F32)
    pick = jnp.concatenate([jnp.where(block == float(b), hit, 0.0).astype(BF) for b in range(2 * PIECES)], axis=1)
    rows = dot(pick, table[...]) * scale
    out[g * GRP : (g + 1) * GRP] = rows.astype(BF).reshape(GRP, PEER, LANES)


def unpack_rows(perm, rows, first, second, start=0, stop=NEXP // GRP):
    def one(g, carry):
        z = dot(perm[...], rows[pl.ds(g * GRP, GRP)].reshape(GROWS, LANES)).astype(BF)
        at = pl.ds(pl.multiple_of(g * GSLOTS, GSLOTS), GSLOTS)
        for kind, ref in enumerate((first, second)):
            for piece in range(PIECES):
                o = (kind * PIECES + piece) * GSLOTS
                ref[at, piece * LANES : (piece + 1) * LANES] = z[o : o + GSLOTS]
        return carry

    lax.fori_loop(start, stop, one, 0)


def pack_rows(perm, out, first, second, start, stop):
    def one(g, carry):
        at = pl.ds(pl.multiple_of(g * GSLOTS, GSLOTS), GSLOTS)
        z = [ref[at, piece * LANES : (piece + 1) * LANES] for ref in (first, second) for piece in range(PIECES)]
        packed = dot(perm[...], jnp.concatenate(z, axis=0), 0, 0)
        out[pl.ds(g * GRP, GRP)] = packed.astype(BF).reshape(GRP, PEER, LANES)
        return carry

    lax.fori_loop(start, stop, one, 0)


def layer_kernel(
    tok, grad, ids, sc, wg, wu, wd, perm_h,
    out, own_out, frm,
    bsem, xs, xr, loc, ws, wr, rs_s, rs_r,
    tv, gv, iv, sv, table, perm, x, rows, fg, fu, fd, xt, xc, xo, xi, hid, gg, ug, part, rel,
):
    me, y, *_ = place()
    up, dn, far = (y + 1) % 4, (y + 3) % 4, (y + 2) % 4
    tos = (up, dn)
    shards, fulls = (wg, wu, wd), (fg, fu, fd)
    span = lambda who, off, n: pl.ds(pl.multiple_of(who * SH + off, 32), n)
    loads = [
        pltpu.make_async_copy(s, d, loc.at[i])
        for i, (s, d) in enumerate(((ids, iv), (sc, sv), (tok, tv), (grad, gv), (perm_h, perm)))
    ]
    mine = [pltpu.make_async_copy(s, f.at[span(y, 0, SH)], loc.at[5 + m]) for m, (s, f) in enumerate(zip(shards, fulls))]
    for q in loads + mine:
        q.start()
    first, relay = [], []

    def gather():
        for m, (s, f) in enumerate(zip(shards, fulls)):
            for way, to in enumerate(tos):
                q = remote(s, f.at[span(y, 0, SH)], ws.at[way, m], wr.at[way, m], (me, to))
                q.start()
                first.append((m, way, q))

    def pack(i):
        if i == 0:
            for q in loads:
                q.wait()
            for piece in range(PIECES):
                lanes = slice(piece * LANES, (piece + 1) * LANES)
                table[piece * TOK : (piece + 1) * TOK, :] = tv[:, lanes]
                table[(PIECES + piece) * TOK : (PIECES + piece + 1) * TOK, :] = gv[:, lanes]
        ids_t = iv[...].astype(F32)
        for g in ((0,), (1, 2), (3, 4), (5, 6), (7,), ())[i]:
            pack_group(g, ids_t, columns(ids_t), sv[...], x, table)

    barrier(bsem, gather, pack)
    own = start_exchange(x, rows, xs.at[0], xr.at[0], loc.at[8])
    for m, way, q in first:
        q.wait_recv()
        p = fulls[m].at[span(tos[1 - way], way * HALF, HALF)]
        r = remote(p, p, ws.at[2 + way, m], wr.at[2 + way, m], (me, tos[way]))
        r.start()
        relay.append(r)
    finish_exchange(x, rows, xs.at[0], xr.at[0], own)
    unpack_rows(perm, rows, xt, xc)
    for q in relay:
        q.wait()
    for _, _, q in first:
        q.wait_send()
    for q in mine:
        q.wait()

    def units(i, carry):
        at = pl.ds(pl.multiple_of(i * FCHUNK, FCHUNK), FCHUNK)
        gate = dot(fg[at, :], xt[...], 1, 1)
        upp = dot(fu[at, :], xt[...], 1, 1)
        hg = dot(fd[at, :], xc[...], 1, 1)
        s = jax.nn.sigmoid(gate)
        act = gate * s
        hid[at, :] = (act * upp).astype(BF)
        gg[at, :] = (hg * upp * (s * (1.0 + gate * (1.0 - s)))).astype(BF)
        ug[at, :] = (hg * act).astype(BF)
        return carry

    lax.fori_loop(0, FF // FCHUNK, units, 0)

    def gradients(who):
        at = span(who, 0, SH)
        part[0, at, :] = dot(gg[at, :], xt[...]).astype(BF)
        part[1, at, :] = dot(ug[at, :], xt[...]).astype(BF)
        part[2, at, :] = dot(hid[at, :], xc[...]).astype(BF)

    def send(m, way, src, dst, row):
        q = remote(src, dst, rs_s.at[row + way, m], rs_r.at[row + way, m], (me, tos[way]))
        q.start()
        return q

    gradients(far)
    relays = [
        (m, way, send(m, way, part.at[m, span(far, way * HALF, HALF)], rel.at[way, m], 0)) for m in range(3) for way in range(2)
    ]
    for piece in range(2):
        cols = slice(piece * D // 2, (piece + 1) * D // 2)
        xo[:, cols] = dot(hid[...], fd[:, cols], 0, 0).astype(BF)
        xi[:, cols] = (dot(gg[...], fg[:, cols], 0, 0) + dot(ug[...], fu[:, cols], 0, 0)).astype(BF)
    pack_rows(perm, x, xo, xi, 0, NEXP // GRP)
    own = start_exchange(x, out, xs.at[1], xr.at[1], loc.at[9])
    gradients(up)
    gradients(dn)
    directs = []
    for m in range(3):
        for way in range(2):
            off = (1 - way) * HALF
            directs.append(send(m, way, part.at[m, span(tos[way], off, HALF)], frm.at[way, m, pl.ds(off, HALF)], 2))
    gradients(y)
    keep = pltpu.make_async_copy(part.at[:, span(y, 0, SH)], own_out, loc.at[10])
    keep.start()
    sums = []
    for m, way, q in relays:
        q.wait_recv()
        off = way * HALF

        def add_rows(r, carry):
            at = span(tos[way], off + r * 32, 32)
            total = part[m, at, :].astype(F32) + rel[way, m, pl.ds(pl.multiple_of(r * 32, 32), 32), :].astype(F32)
            part[m, at, :] = total.astype(BF)
            return carry

        lax.fori_loop(0, HALF // 32, add_rows, 0)
        sums.append(send(m, way, part.at[m, span(tos[way], off, HALF)], frm.at[way, m, pl.ds(off, HALF)], 4))
    for q in directs:
        q.wait()
    for q in sums:
        q.wait()
    for _, _, q in relays:
        q.wait_send()
    keep.wait()
    finish_exchange(x, out, xs.at[1], xr.at[1], own)


def combine_kernel(
    rows_h, frm_h, own_h, perm_h, grad_h, ids_h, sc_h,
    out, dtok, dsc, og, ou, od,
    rows, frm, perm, grad, ids, sc, xo, xi, own, fin, sem, rsem,
):
    outs = (og, ou, od)
    small = [
        pltpu.make_async_copy(s, d, sem.at[6 + i])
        for i, (s, d) in enumerate(((perm_h, perm), (grad_h, grad), (ids_h, ids), (sc_h, sc)))
    ]
    span = 2 * GRP
    chunks = [
        pltpu.make_async_copy(rows_h.at[pl.ds(i * span, span)], rows.at[pl.ds(i * span, span)], rsem.at[i]) for i in range(4)
    ]
    load = [
        [
            pltpu.make_async_copy(own_h.at[m], own.at[m], sem.at[m]),
            pltpu.make_async_copy(frm_h.at[0, m], frm.at[0, m], sem.at[10 + m]),
            pltpu.make_async_copy(frm_h.at[1, m], frm.at[1, m], sem.at[13 + m]),
        ]
        for m in range(3)
    ]
    store = [pltpu.make_async_copy(fin.at[m], o, sem.at[3 + m]) for m, o in enumerate(outs)]
    for q in small + chunks + sum(load, []):
        q.start()
    for q in small:
        q.wait()
    for i in range(4):
        chunks[i].wait()
        unpack_rows(perm, rows, xo, xi, 2 * i, 2 * i + 2)
    for m in range(3):
        for q in load[m]:
            q.wait()

        def final(r, carry):
            at = pl.ds(pl.multiple_of(r * 32, 32), 32)
            total = own[m, at, :].astype(F32) + frm[0, m, at, :].astype(F32)
            fin[m, at, :] = (total + frm[1, m, at, :].astype(F32)).astype(BF)
            return carry

        lax.fori_loop(0, SH // 32, final, 0)
        store[m].start()
    ids_t = ids[...].astype(F32)
    t0, t1 = targets_col(columns(ids_t), ids_t)
    slot = lax.broadcasted_iota(I32, (TOK, SLOTS), 1).astype(F32)
    g0 = (t0 == slot).astype(F32).astype(BF)
    g1 = (t1 == slot).astype(F32).astype(BF)
    both = g0 + g1
    sc_c = columns(sc[...])
    s0, s1 = sc_c[:, 0:1], sc_c[:, 1:2]
    d0 = jnp.zeros((TOK, 1), F32)
    d1 = jnp.zeros((TOK, 1), F32)
    for piece in range(PIECES):
        lanes = slice(piece * LANES, (piece + 1) * LANES)
        p0 = dot(g0, xo[:, lanes])
        p1 = dot(g1, xo[:, lanes])
        cot = grad[:, lanes].astype(F32)
        out[:, lanes] = (s0 * p0 + s1 * p1).astype(BF)
        d0 += jnp.sum(cot * p0, axis=1, keepdims=True)
        d1 += jnp.sum(cot * p1, axis=1, keepdims=True)
        dtok[:, lanes] = dot(both, xi[:, lanes]).astype(BF)
    dsc[...] = jnp.concatenate([d0, d1] * 4, axis=1).T[0:2, :]
    for q in store:
        q.wait()


def shards(tokens, expert_ids, gate_scores, gate_proj, up_proj, down_proj, out_grad):
    sd, vmem = jax.ShapeDtypeStruct, pltpu.VMEM
    vm = pl.BlockSpec(memory_space=pltpu.VMEM)
    anyw = pl.BlockSpec(memory_space=pl.ANY)
    dma, reg = pltpu.SemaphoreType.DMA, pltpu.SemaphoreType.REGULAR
    ids_t, sc_t = expert_ids.T, gate_scores.T
    perm = jnp.asarray(PERM, BF)
    blocks = (NEXP, PEER, LANES)
    returned, own, frm = pl.pallas_call(
        layer_kernel,
        name="layer",
        out_shape=(sd(blocks, BF), sd((3, SH, D), BF), sd((2, 3, SH, D), BF)),
        in_specs=[anyw] * 8,
        out_specs=(anyw,) * 3,
        scratch_shapes=[reg((6,)), dma((2,)), dma((2,)), dma((11,)), dma((4, 3)), dma((4, 3)), dma((6, 3)), dma((6, 3))]
        + [vmem((TOK, D), BF)] * 2
        + [vmem((2, TOK), I32), vmem((2, TOK), F32), vmem((2 * PIECES * TOK, LANES), BF), vmem((GROWS, GROWS), BF)]
        + [vmem(blocks, BF)] * 2
        + [vmem((FF, D), BF)] * 3
        + [vmem((SLOTS, D), BF)] * 4
        + [vmem((FF, SLOTS), BF)] * 3
        + [vmem((3, FF, D), BF), vmem((2, 3, HALF, D), BF)],
        compiler_params=pltpu.CompilerParams(collective_id=1, has_side_effects=True, vmem_limit_bytes=63 << 20),
    )(tokens, out_grad, ids_t, sc_t, gate_proj[0], up_proj[0], down_proj[0], perm)
    output, d_tokens, d_scores_t, gg, gu, gd = pl.pallas_call(
        combine_kernel,
        name="combine",
        out_shape=(sd((TOK, D), BF), sd((TOK, D), BF), sd((2, TOK), F32)) + (sd((SH, D), BF),) * 3,
        in_specs=[anyw] * 7,
        out_specs=(vm,) * 3 + (anyw,) * 3,
        scratch_shapes=[vmem(blocks, BF), vmem((2, 3, SH, D), BF), vmem((GROWS, GROWS), BF), vmem((TOK, D), BF)]
        + [vmem((2, TOK), I32), vmem((2, TOK), F32)]
        + [vmem((SLOTS, D), BF)] * 2
        + [vmem((3, SH, D), BF)] * 2
        + [dma((16,)), dma((4,))],
        compiler_params=pltpu.CompilerParams(vmem_limit_bytes=62 << 20),
    )(returned, frm, own, perm, out_grad, ids_t, sc_t)
    return output, d_tokens, d_scores_t.T, gg[None], gu[None], gd[None]


def solution(mesh):
    rows, weights = P(("expert", "dp"), None), P("expert", "dp", None)
    return jax.shard_map(
        shards,
        mesh=mesh,
        in_specs=(rows, rows, rows, weights, weights, weights, rows),
        out_specs=(rows, rows, rows, weights, weights, weights),
        check_vma=False,
    )
```
